32 devices in a mesh: req: 8 (over z, x), tp: 4 (over y, core).
Axes of the slice: x: 2, y: 2, z: 4, core: 2. Of those that a mesh axis runs over, the one named last changes fastest.
Arguments:
- hidden_in: bfloat16 [8, 1024, 2048], P('req', None, 'tp'), may hold values from -6 to 6
- ln_gain: float32 [2048], replicated, may hold values from 0.25 to 1.75
- ln_bias: float32 [2048], replicated, may hold values from -1.5 to 1.5
- w_qkv: bfloat16 [3, 2048, 2048], P(None, None, 'tp'), may hold values from -0.125 to 0.125
- b_qkv: float32 [3, 2048], P(None, 'tp'), may hold values from -1.5 to 1.5
- w_out: bfloat16 [2048, 2048], P('tp'), may hold values from -0.125 to 0.125
- b_out: float32 [2048], replicated, may hold values from -1.5 to 1.5
- alibi_slope: float32 [16], P('tp'), may hold values from 2.4414063e-05 to 0.1
- prefix_k: bfloat16 [2048, 2048], P('req', 'tp'), may hold values from -160 to 160
- prefix_v: bfloat16 [2048, 2048], P('req', 'tp'), may hold values from -6 to 6
- suffix_len: int32 [8], P('req'), may hold values from 64 to 1024, as said below
- group_of: int32 [8], P('req'), may hold values from 0 to 1
- block_of_device: int32 [8], P('req'), may hold values from 0 to 7, each once
Outputs:
- mixed: bfloat16 [8, 1024, 2048], P('req', None, 'tp')
- cache_k: bfloat16 [8, 1024, 2048], P('req', None, 'tp')
- cache_v: bfloat16 [8, 1024, 2048], P('req', None, 'tp')
The draws below stay inside these ranges and needn't reach their ends.
Inputs may be any that keep to these rules, and one draw needn't show every extreme that they name: `suffix_len`: every request has at least 64 live slots; some request has exactly 1024.
All inputs are finite; a program needn't handle non-finite values.
Results may differ from the reference program's by a relative error of at most 0.011.
Values may be sent and summed in bfloat16 or wider, within the bound.
A program may use at most 384 MiB of HBM per device.

```python
import math
import jax
import jax.numpy as jnp
from jax import lax

D = 2048
H = 16
HD = 128
HH = 2048
SUF = 1024
PB = 256
REQS = 8
PREFIX = 1024
N_REQ = 8
N_TP = 4


def draw_suffix_len(key, part):
    first_key, second_key = jax.random.split(jax.random.fold_in(key, 11))
    lengths = jax.random.randint(first_key, (N_REQ,), SUF // 16, SUF + 1)
    chosen = jax.random.randint(second_key, (), 0, N_REQ)
    return jnp.where(jnp.arange(N_REQ) == chosen, SUF, lengths).astype(jnp.int32)


def draw_prefix_k(key, part):
    base = jax.random.normal(jax.random.fold_in(key, 23), (N_REQ * PB, HH), jnp.float32)
    base = jnp.clip(base, -6.0, 6.0)
    return jnp.clip(base, -160.0, 160.0).astype(jnp.bfloat16)


def plant(array, own_key, smallest, high):
    spot = [jax.random.randint(jax.random.fold_in(own_key, axis), (), 0, length) for axis, length in enumerate(array.shape)]
    widest = array.shape.index(max(array.shape))
    neighbour = spot[:widest] + [(spot[widest] + 1) % array.shape[widest]] + spot[widest + 1:]
    return array.at[tuple(spot)].set(smallest).at[tuple(neighbour)].set(high)


def levels(rng, extent, shards, least, high):
    def one(position, shards_of):
        steps = jax.random.uniform(jax.random.fold_in(jax.random.fold_in(rng, 6), position), (shards_of,), jnp.float32, least / len(shards), high / len(shards))
        return jnp.repeat(jnp.exp(steps), extent[position] // shards_of).reshape((-1,) + (1,) * (len(extent) - position - 1))

    level = one(*shards[0])
    for cut in shards[1:]:
        level = level * one(*cut)
    return level


def noise(key, shape, scale, bound, shards=(), held_as=jnp.bfloat16):
    level = levels(key, shape, shards, -0.22, 0.18) if shards else 1.0
    entries = jax.random.normal(key, shape, jnp.float32) * scale * level
    return jnp.minimum(jnp.maximum(entries, -bound), bound).astype(held_as)


def setup_inputs(seed: int = 0) -> dict:
    streams_of = jax.random.split(jax.random.key(seed), 14)
    return {
        "hidden_in": noise(streams_of[0], (REQS, SUF, D), 1.0, 6.0, ((0, 8), (2, 4))),
        "ln_gain": jnp.clip(1.0 + 0.15 * jax.random.normal(streams_of[1], (D,), jnp.float32), 0.25, 1.75),
        "ln_bias": noise(streams_of[2], (D,), 0.3, 1.5, (), jnp.float32),
        "w_qkv": noise(streams_of[3], (3, D, HH), D ** -0.5, 0.125, ((2, 4),)),
        "b_qkv": noise(streams_of[4], (3, HH), 0.3, 1.5, ((1, 4),), jnp.float32),
        "w_out": noise(streams_of[5], (HH, D), HH ** -0.5, 0.125, ((0, 4),)),
        "b_out": noise(streams_of[6], (D,), 0.3, 1.5, (), jnp.float32),
        "alibi_slope": jnp.clip(jnp.exp(math.log(0.1) - 8.317766 * jax.random.uniform(streams_of[7], (H,), jnp.float32) ** levels(streams_of[7], (H,), ((0, 4),), -0.2, 0.2)), 2.441406286379788e-05, 0.1),
        "prefix_k": draw_prefix_k(jax.random.fold_in(streams_of[13], 71), 0),
        "prefix_v": noise(streams_of[9], (N_REQ * PB, HH), 1.0, 6.0, ((0, 8), (1, 4))),
        "suffix_len": draw_suffix_len(jax.random.fold_in(streams_of[13], 71), 0),
        "group_of": plant(jax.random.randint(streams_of[11], (REQS,), 0, 2), jax.random.fold_in(streams_of[11], 1), 0, 1).astype(jnp.int32),
        "block_of_device": jax.random.permutation(streams_of[12], N_REQ).astype(jnp.int32),
    }


EPS = 1e-05
NEGATIVE = -1e+30

def reference(hidden_in, ln_gain, ln_bias, w_qkv, b_qkv, w_out, b_out, alibi_slope, prefix_k, prefix_v, suffix_len, group_of, block_of_device):
    holders = jnp.zeros((N_REQ,), jnp.int32).at[block_of_device].set(jnp.arange(N_REQ, dtype=jnp.int32))
    ordered_k = prefix_k.reshape(N_REQ, PB, HH)[holders].reshape(2, PREFIX, HH)
    ordered_v = prefix_v.reshape(N_REQ, PB, HH)[holders].reshape(2, PREFIX, HH)
    slot_ids = jnp.arange(SUF, dtype=jnp.int32)
    key_pos = jnp.concatenate([jnp.arange(PREFIX, dtype=jnp.int32), PREFIX + slot_ids])
    query_pos = PREFIX + slot_ids
    distance = (query_pos[:, None] - key_pos[None, :]).astype(jnp.float32)
    group_width = HH // N_TP
    out_groups = w_out.reshape(N_TP, group_width, D).astype(jnp.float32)

    def one_request(inputs):
        slot_rows, length, group = inputs
        values32 = slot_rows.astype(jnp.float32)
        center = values32 - lax.optimization_barrier(jnp.mean(values32, axis=1, keepdims=True))
        spread = lax.optimization_barrier(jnp.mean(center * center, axis=1, keepdims=True))
        normed = (center / jnp.sqrt(spread + EPS) * ln_gain + ln_bias).astype(jnp.bfloat16)
        projected = jnp.einsum('sd,cdh->csh', normed.astype(jnp.float32), w_qkv.astype(jnp.float32)) + b_qkv[:, None, :]
        projected = projected.astype(jnp.bfloat16)
        query, keys, values = (projected[0], projected[1], projected[2])
        live = slot_ids < length
        keys_out = jnp.where(live[:, None], keys, jnp.zeros_like(keys))
        values_out = jnp.where(live[:, None], values, jnp.zeros_like(values))
        all_keys = jnp.concatenate([ordered_k[group], keys], axis=0)
        all_values = jnp.concatenate([ordered_v[group], values], axis=0)
        allowed = (key_pos[None, :] < PREFIX) | (key_pos[None, :] <= query_pos[:, None]) & (key_pos[None, :] < PREFIX + length)
        query_heads = query.reshape(SUF, H, HD).astype(jnp.float32)
        key_heads = all_keys.reshape(PREFIX + SUF, H, HD).astype(jnp.float32)
        value_heads = all_values.reshape(PREFIX + SUF, H, HD).astype(jnp.float32)
        scores = jnp.einsum('shd,khd->hsk', query_heads, key_heads) / jnp.sqrt(jnp.float32(HD))
        scores = scores - alibi_slope[:, None, None] * distance[None, :, :]
        scores = jnp.where(allowed[None], scores, NEGATIVE)
        row_top = lax.optimization_barrier(jnp.max(scores, axis=2, keepdims=True))
        weights = jnp.where(allowed[None], jnp.exp(scores - row_top), 0.0)
        total = lax.optimization_barrier(jnp.sum(weights, axis=2))
        rounded = lax.optimization_barrier(weights.astype(jnp.bfloat16)).astype(jnp.float32)
        attended = jnp.einsum('hsk,khd->hsd', rounded, value_heads) / total[:, :, None]
        attended = attended.transpose(1, 0, 2).reshape(SUF, HH).astype(jnp.bfloat16)
        parts = attended.reshape(SUF, N_TP, group_width).astype(jnp.float32)
        partial_value = jnp.einsum('sgf,gfd->gsd', parts, out_groups)
        partial_value = lax.optimization_barrier(partial_value.astype(jnp.bfloat16)).astype(jnp.float32)
        result = lax.optimization_barrier(jnp.sum(partial_value, axis=0)) + b_out + values32
        result = jnp.where(live[:, None], result, 0.0).astype(jnp.bfloat16)
        return (result, keys_out, values_out)
    mixed, cache_k, cache_v = lax.map(one_request, (hidden_in, suffix_len, group_of))
    return (mixed, cache_k, cache_v)
```

```python
import functools
import math

import jax
import jax.numpy as jnp
from jax import lax
from jax.experimental import pallas as pl
from jax.experimental.pallas import tpu as pltpu
from jax.sharding import PartitionSpec as P

EPS = 1e-05
NEGATIVE = -1e30
LOG2E = math.log2(math.e)
ROWS = 256
F32 = jnp.float32
BF16 = jnp.bfloat16


def dot_t(a, b):
    return lax.dot_general(a, b, (((1,), (1,)), ((), ())), preferred_element_type=F32)


def kernel(
    n_req,
    n_x,
    order,
    length_ref,
    slope,
    hid,
    gain,
    beta,
    w_qkv,
    b_qkv,
    w_out,
    b_out,
    pk,
    pv,
    mixed,
    ck,
    cv,
    hbuf,
    wq,
    wo,
    nrm,
    qkv,
    cst,
    kv,
    acc,
    mst,
    lst,
    att,
    pbuf,
    sibr,
    ys,
    yr,
    ost,
    loc_sem,
    out_sem,
    hs,
    hr,
    zs,
    xs,
    kvr,
    ss,
    sr,
    yss,
    yrs,
):
    slots, width = hid.shape[1], hid.shape[2]
    block = pk.shape[0]
    heads, size = qkv.shape[1], qkv.shape[3]
    n_rc = slots // ROWS
    n_z = n_req // n_x
    nb = n_req // 2
    prefix = nb * block
    feats = 4 * width

    r = lax.axis_index("req")
    t = lax.axis_index("tp")
    y, c = t // 2, t % 2
    sib = y * 2 + (1 - c)
    oth = (1 - y) * 2 + c
    far = (1 - y) * 2 + (1 - c)
    z, x = r // n_x, r % n_x
    x_peers = [z * n_x + (x + d) % n_x for d in range(1, n_x)]

    def remote(src, dst, send, recv, dev):
        return pltpu.make_async_remote_copy(
            src_ref=src,
            dst_ref=dst,
            send_sem=send,
            recv_sem=recv,
            device_id=dev,
            device_id_type=pl.DeviceIdType.MESH,
        )

    barrier = pltpu.get_barrier_semaphore()

    def greet(dev):
        pl.semaphore_signal(
            barrier, inc=1, device_id=dev, device_id_type=pl.DeviceIdType.MESH
        )

    greet((r, sib))
    greet((r, oth))
    for peer in x_peers:
        greet((peer, t))

    @pl.when(z > 0)
    def _():
        greet((r - n_x, t))

    @pl.when(z < n_z - 1)
    def _():
        greet((r + n_x, t))

    below, above = (z + n_z - 1) // n_z, (2 * n_z - 2 - z) // n_z
    pl.semaphore_wait(barrier, 2 + len(x_peers) + below + above)

    def rows_of(i):
        return pl.ds(pl.multiple_of(i * ROWS, ROWS), ROWS)

    def h_other(i):
        rows = rows_of(i)
        return remote(
            hid.at[0, rows], hbuf.at[t, rows], hs.at[0, i], hr.at[0, i], (r, oth)
        )

    def h_sib(i):
        rows = rows_of(i)
        return remote(
            hid.at[0, rows], hbuf.at[t, rows], hs.at[1, i], hr.at[1, i], (r, sib)
        )

    def h_fwd(i):
        rows = rows_of(i)
        return remote(
            hbuf.at[oth, rows], hbuf.at[oth, rows], hs.at[2, i], hr.at[2, i], (r, sib)
        )

    def up(src, a, zj):
        return remote(
            src, kv.at[a, zj * n_x + x], zs.at[0, a, zj], kvr.at[a, zj * n_x + x], (r + n_x, t)
        )

    def down(src, a, zj):
        return remote(
            src, kv.at[a, zj * n_x + x], zs.at[1, a, zj], kvr.at[a, zj * n_x + x], (r - n_x, t)
        )

    def across(src, a, zj, d):
        return remote(
            src,
            kv.at[a, zj * n_x + x],
            xs.at[d, a, zj],
            kvr.at[a, zj * n_x + x],
            (x_peers[d], t),
        )

    def kv_wait(a, j):
        remote(kv.at[a, j], kv.at[a, j], hs.at[0, 0], kvr.at[a, j], (r, sib)).wait_recv()

    for i in range(n_rc):
        h_other(i).start()
        h_sib(i).start()
    own = [pltpu.make_async_copy(hid.at[0], hbuf.at[t], loc_sem.at[0])]
    own.append(pltpu.make_async_copy(w_qkv, wq, loc_sem.at[1]))
    own.append(pltpu.make_async_copy(w_out, wo, loc_sem.at[2]))
    own.append(pltpu.make_async_copy(pk, kv.at[0, r], loc_sem.at[3]))
    own.append(pltpu.make_async_copy(pv, kv.at[1, r], loc_sem.at[4]))
    for a, src in ((0, pk), (1, pv)):

        @pl.when(z < n_z - 1)
        def _(a=a, src=src):
            up(src, a, z).start()

        @pl.when(z > 0)
        def _(a=a, src=src):
            down(src, a, z).start()

        for d in range(n_x - 1):
            across(src, a, z, d).start()
    for copy in own:
        copy.start()

    n_events = 2 * (n_z - 1)

    def handle(e):
        s, a = e // 2 + 1, e % 2

        @pl.when(z - s >= 0)
        def _():
            zj = z - s
            here = kv.at[a, zj * n_x + x]
            kv_wait(a, zj * n_x + x)

            @pl.when(z < n_z - 1)
            def _():
                up(here, a, zj).start()

            for d in range(n_x - 1):
                across(here, a, zj, d).start()

        @pl.when(z + s < n_z)
        def _():
            zj = z + s
            here = kv.at[a, zj * n_x + x]
            kv_wait(a, zj * n_x + x)

            @pl.when(z > 0)
            def _():
                down(here, a, zj).start()

            for d in range(n_x - 1):
                across(here, a, zj, d).start()

    length = length_ref[0]

    def live(i):
        ids = lax.broadcasted_iota(jnp.int32, (ROWS, width), 0) + i * ROWS
        return ids < length

    def cache_out(i, j):
        rows = rows_of(i)
        dst = (ck, cv)[j]
        return pltpu.make_async_copy(cst.at[j, rows], dst.at[0, rows], out_sem.at[j, i])

    own[0].wait()
    own[1].wait()

    def project(i, carry):
        rows = rows_of(i)
        h_other(i).wait_recv()
        h_fwd(i).start()
        h_sib(i).wait_recv()
        h_fwd(i).wait_recv()
        pieces = [hbuf[f, rows, :].astype(F32) for f in range(4)]
        mean = sum(jnp.sum(p, axis=1, keepdims=True) for p in pieces) * (1.0 / feats)
        pieces = [p - mean for p in pieces]
        var = sum(jnp.sum(p * p, axis=1, keepdims=True) for p in pieces) * (1.0 / feats)
        inv = 1.0 / jnp.sqrt(var + EPS)
        for f in range(4):
            cols = slice(f * width, (f + 1) * width)
            nrm[:, cols] = (pieces[f] * inv * gain[:, cols] + beta[:, cols]).astype(BF16)
        keep = live(i)
        for j in range(3):
            out = jnp.dot(nrm[...], wq[j], preferred_element_type=F32) + b_qkv[j : j + 1, :]
            out = out.astype(BF16)
            for h in range(heads):
                qkv[j, h, rows, :] = out[:, h * size : (h + 1) * size]
            if j > 0:
                cst[j - 1, rows, :] = jnp.where(keep, out, jnp.zeros_like(out))
                cache_out(i, j - 1).start()

        @pl.when(i < n_events)
        def _():
            handle(i)

        return carry

    lax.fori_loop(0, n_rc, project, 0)

    scale2 = LOG2E / math.sqrt(size)
    tri = lax.broadcasted_iota(jnp.int32, (ROWS, ROWS), 1) <= lax.broadcasted_iota(
        jnp.int32, (ROWS, ROWS), 0
    )

    def suffix(h, carry):
        slope2 = slope[h] * LOG2E
        ids = lax.broadcasted_iota(jnp.int32, (1, slots), 1)
        shift = jnp.where(ids < length, ids.astype(F32) * slope2, NEGATIVE)
        for i in range(n_rc):
            lo, hi = i * ROWS, (i + 1) * ROWS
            q = qkv[0, h, lo:hi, :]
            sd = dot_t(q, qkv[1, h, lo:hi, :]) * scale2 + shift[:, lo:hi]
            sd = jnp.where(tri, sd, NEGATIVE)
            m = jnp.max(sd, axis=1, keepdims=True)
            if i > 0:
                so = dot_t(q, qkv[1, h, 0:lo, :]) * scale2 + shift[:, 0:lo]
                m = jnp.maximum(m, jnp.max(so, axis=1, keepdims=True))
            wd = jnp.exp2(sd - m)
            total = jnp.sum(wd, axis=1, keepdims=True)
            out = jnp.dot(
                wd.astype(BF16), qkv[2, h, lo:hi, :], preferred_element_type=F32
            )
            if i > 0:
                wo_ = jnp.exp2(so - m)
                total = total + jnp.sum(wo_, axis=1, keepdims=True)
                out = out + jnp.dot(
                    wo_.astype(BF16), qkv[2, h, 0:lo, :], preferred_element_type=F32
                )
            acc[h, lo:hi, :] = out
            mst[h, lo:hi, :] = jnp.broadcast_to(m, (ROWS, size))
            lst[h, lo:hi, :] = jnp.broadcast_to(total, (ROWS, size))

        @pl.when(n_rc + h < n_events)
        def _():
            handle(n_rc + h)

        return carry

    lax.fori_loop(0, heads, suffix, 0)

    def late(e, carry):
        handle(e)
        return carry

    if n_events > n_rc + heads:
        lax.fori_loop(n_rc + heads, n_events, late, 0)

    for copy in own[2:]:
        copy.wait()

    def wait_across(zj, carry):
        for a in range(2):
            for d in range(1, n_x):
                kv_wait(a, zj * n_x + (x + d) % n_x)
        return carry

    lax.fori_loop(0, n_z, wait_across, 0)

    def to_sib(i):
        return remote(pbuf.at[i, 1 - c], sibr.at[i], ss.at[i], sr.at[i], (r, sib))

    def to_oth(i):
        return remote(ys.at[i], yr.at[i], yss.at[i], yrs.at[i], (r, oth))

    step = min(4, nb)

    def finish(i, carry):
        rows = rows_of(i)
        for h in range(heads):
            slope2 = slope[h] * LOG2E
            cols = slice(h * size, (h + 1) * size)
            q = qkv[0, h, rows, :]
            m = mst[h, rows, :][:, :1]
            total = lst[h, rows, :][:, :1]
            out = acc[h, rows, :]
            for b0 in range(0, nb, step):
                holders = [order[b] for b in range(b0, b0 + step)]
                keys = jnp.concatenate([kv[0, j, :, cols] for j in holders], axis=0)
                vals = jnp.concatenate([kv[1, j, :, cols] for j in holders], axis=0)
                ids = lax.broadcasted_iota(jnp.int32, (1, step * block), 1)
                shift = (ids + (b0 * block - prefix)).astype(F32) * slope2
                sc = dot_t(q, keys) * scale2 + shift
                new = jnp.maximum(m, jnp.max(sc, axis=1, keepdims=True))
                fac = jnp.exp2(m - new)
                w = jnp.exp2(sc - new)
                total = total * fac + jnp.sum(w, axis=1, keepdims=True)
                out = out * fac + jnp.dot(w.astype(BF16), vals, preferred_element_type=F32)
                m = new
            att[:, cols] = (out / total).astype(BF16)
        for f in range(4):
            part = jnp.dot(
                att[...], wo[:, f * width : (f + 1) * width], preferred_element_type=F32
            )
            pbuf[i, f % 2, f // 2] = part.astype(BF16)
        to_sib(i).start()
        to_sib(i).wait_recv()
        ys[i] = (pbuf[i, c, 1 - y].astype(F32) + sibr[i, 1 - y].astype(F32)).astype(BF16)
        to_oth(i).start()
        return carry

    lax.fori_loop(0, n_rc, finish, 0)

    def mixed_out(i):
        rows = rows_of(i)
        return pltpu.make_async_copy(ost.at[rows], mixed.at[0, rows], out_sem.at[2, i])

    def final(i, carry):
        rows = rows_of(i)
        to_oth(i).wait_recv()
        out = pbuf[i, c, y].astype(F32) + sibr[i, y].astype(F32) + yr[i].astype(F32)
        out = out + b_out[t] + hbuf[t, rows, :].astype(F32)
        ost[rows, :] = jnp.where(live(i), out, 0.0).astype(BF16)
        mixed_out(i).start()
        return carry

    lax.fori_loop(0, n_rc, final, 0)

    def drain(i, carry):
        h_other(i).wait_send()
        h_sib(i).wait_send()
        h_fwd(i).wait_send()
        to_sib(i).wait_send()
        to_oth(i).wait_send()
        cache_out(i, 0).wait()
        cache_out(i, 1).wait()
        mixed_out(i).wait()
        return carry

    lax.fori_loop(0, n_rc, drain, 0)

    def drain_prefix(zj, carry):
        for a in range(2):
            here = kv.at[a, zj * n_x + x]

            @pl.when(jnp.logical_and(zj <= z, z < n_z - 1))
            def _():
                up(here, a, zj).wait_send()

            @pl.when(jnp.logical_and(zj >= z, z > 0))
            def _():
                down(here, a, zj).wait_send()

            for d in range(n_x - 1):
                across(here, a, zj, d).wait_send()
        return carry

    lax.fori_loop(0, n_z, drain_prefix, 0)


def on_device(
    n_req,
    n_x,
    hidden_in,
    ln_gain,
    ln_bias,
    w_qkv,
    b_qkv,
    w_out,
    b_out,
    alibi_slope,
    prefix_k,
    prefix_v,
    suffix_len,
    group_of,
    block_of_device,
):
    _, slots, width = hidden_in.shape
    heads = alibi_slope.shape[0]
    size = w_qkv.shape[2] // heads
    block = prefix_k.shape[0]
    nb = n_req // 2
    n_rc = slots // ROWS
    n_z = n_req // n_x
    numbers = lax.all_gather(block_of_device, "req", axis=0, tiled=True)
    wanted = group_of[0] * nb + lax.iota(jnp.int32, nb)
    match = numbers[None, :] == wanted[:, None]
    order = jnp.sum(jnp.where(match, lax.iota(jnp.int32, n_req)[None, :], 0), axis=1)
    smem = pl.BlockSpec(memory_space=pltpu.SMEM)
    vmem = pl.BlockSpec(memory_space=pltpu.VMEM)
    hbm = pl.BlockSpec(memory_space=pl.ANY)
    dma = pltpu.SemaphoreType.DMA
    cache = jax.ShapeDtypeStruct((1, slots, width), BF16)
    return pl.pallas_call(
        functools.partial(kernel, n_req, n_x),
        out_shape=(cache, cache, cache),
        in_specs=[smem, smem, smem, hbm, vmem, vmem, hbm, vmem, hbm, vmem, hbm, hbm],
        out_specs=(hbm, hbm, hbm),
        scratch_shapes=[
            pltpu.VMEM((4, slots, width), BF16),
            pltpu.VMEM(w_qkv.shape, BF16),
            pltpu.VMEM(w_out.shape, BF16),
            pltpu.VMEM((ROWS, 4 * width), BF16),
            pltpu.VMEM((3, heads, slots, size), BF16),
            pltpu.VMEM((2, slots, width), BF16),
            pltpu.VMEM((2, n_req, block, heads * size), BF16),
            pltpu.VMEM((heads, slots, size), F32),
            pltpu.VMEM((heads, slots, size), F32),
            pltpu.VMEM((heads, slots, size), F32),
            pltpu.VMEM((ROWS, heads * size), BF16),
            pltpu.VMEM((n_rc, 2, 2, ROWS, width), BF16),
            pltpu.VMEM((n_rc, 2, ROWS, width), BF16),
            pltpu.VMEM((n_rc, ROWS, width), BF16),
            pltpu.VMEM((n_rc, ROWS, width), BF16),
            pltpu.VMEM((slots, width), BF16),
            dma((5,)),
            dma((3, n_rc)),
            dma((3, n_rc)),
            dma((3, n_rc)),
            dma((2, 2, n_z)),
            dma((n_x - 1, 2, n_z)),
            dma((2, n_req)),
            dma((n_rc,)),
            dma((n_rc,)),
            dma((n_rc,)),
            dma((n_rc,)),
        ],
        compiler_params=pltpu.CompilerParams(
            collective_id=0, has_side_effects=True, vmem_limit_bytes=60 << 20
        ),
        name="sublayer",
    )(
        order,
        suffix_len,
        alibi_slope,
        hidden_in,
        ln_gain[None],
        ln_bias[None],
        w_qkv,
        b_qkv,
        w_out,
        b_out.reshape(4, 1, width),
        prefix_k,
        prefix_v,
    )


def solution(mesh):
    n_req = mesh.shape["req"]
    n_x = 2 if n_req <= 8 else 4
    return jax.shard_map(
        functools.partial(on_device, n_req, n_x),
        mesh=mesh,
        in_specs=(
            P("req", None, "tp"),
            P(),
            P(),
            P(None, None, "tp"),
            P(None, "tp"),
            P("tp", None),
            P(),
            P("tp"),
            P("req", "tp"),
            P("req", "tp"),
            P("req"),
            P("req"),
            P("req"),
        ),
        out_specs=(P("req", None, "tp"), P("req", None, "tp"), P("req", None, "tp")),
        check_vma=False,
    )
```

```python
import functools
import math

import jax
import jax.numpy as jnp
from jax import lax
from jax.experimental import pallas as pl
from jax.experimental.pallas import tpu as pltpu
from jax.sharding import PartitionSpec as P

EPS = 1e-05
NEGATIVE = -1e30
LOG2E = math.log2(math.e)
ROWS = 256
F32 = jnp.float32
BF16 = jnp.bfloat16


def dot_t(a, b):
    return lax.dot_general(a, b, (((1,), (1,)), ((), ())), preferred_element_type=F32)


def kernel(
    n_req,
    n_x,
    block_ref,
    group_ref,
    length_ref,
    slope,
    hid,
    gain,
    beta,
    w_qkv,
    b_qkv,
    w_out,
    b_out,
    pk,
    pv,
    mixed,
    ck,
    cv,
    hbuf,
    wq,
    wo,
    nrm,
    qkv,
    cst,
    kv,
    acc,
    mst,
    lst,
    att,
    pbuf,
    sibr,
    ys,
    yr,
    ost,
    ids,
    mine,
    loc_sem,
    out_sem,
    hs,
    hr,
    zs,
    xs,
    kvr,
    ss,
    sr,
    yss,
    yrs,
    ids_send,
    ids_recv,
):
    slots, width = hid.shape[1], hid.shape[2]
    block = pk.shape[0]
    heads, size = qkv.shape[1], qkv.shape[3]
    n_rc = slots // ROWS
    n_z = n_req // n_x
    nb = n_req // 2
    prefix = nb * block
    feats = 4 * width

    r = lax.axis_index("req")
    t = lax.axis_index("tp")
    y, c = t // 2, t % 2
    sib = y * 2 + (1 - c)
    oth = (1 - y) * 2 + c
    far = (1 - y) * 2 + (1 - c)
    z, x = r // n_x, r % n_x
    x_peers = [z * n_x + (x + d) % n_x for d in range(1, n_x)]

    def remote(src, dst, send, recv, dev):
        return pltpu.make_async_remote_copy(
            src_ref=src,
            dst_ref=dst,
            send_sem=send,
            recv_sem=recv,
            device_id=dev,
            device_id_type=pl.DeviceIdType.MESH,
        )

    barrier = pltpu.get_barrier_semaphore()

    def greet(dev):
        pl.semaphore_signal(
            barrier, inc=1, device_id=dev, device_id_type=pl.DeviceIdType.MESH
        )

    greet((r, sib))
    greet((r, oth))

    def greet_req(d, carry):
        greet(((r + d) % n_req, t))
        return carry

    lax.fori_loop(1, n_req, greet_req, 0)
    pl.semaphore_wait(barrier, n_req + 1)

    def number(d):
        return remote(
            mine, ids.at[r], ids_send.at[d], ids_recv.at[r], ((r + d) % n_req, t)
        )

    mine[...] = jnp.full(mine.shape, block_ref[0], jnp.int32)
    ids[r] = jnp.full(mine.shape, block_ref[0], jnp.int32)

    def send_number(d, carry):
        number(d).start()
        return carry

    lax.fori_loop(1, n_req, send_number, 0)

    def rows_of(i):
        return pl.ds(pl.multiple_of(i * ROWS, ROWS), ROWS)

    def h_other(i):
        rows = rows_of(i)
        return remote(
            hid.at[0, rows], hbuf.at[t, rows], hs.at[0, i], hr.at[0, i], (r, oth)
        )

    def h_sib(i):
        rows = rows_of(i)
        return remote(
            hid.at[0, rows], hbuf.at[t, rows], hs.at[1, i], hr.at[1, i], (r, sib)
        )

    def h_fwd(i):
        rows = rows_of(i)
        return remote(
            hbuf.at[oth, rows], hbuf.at[oth, rows], hs.at[2, i], hr.at[2, i], (r, sib)
        )

    def up(src, a, zj):
        return remote(
            src, kv.at[a, zj * n_x + x], zs.at[0, a, zj], kvr.at[a, zj * n_x + x], (r + n_x, t)
        )

    def down(src, a, zj):
        return remote(
            src, kv.at[a, zj * n_x + x], zs.at[1, a, zj], kvr.at[a, zj * n_x + x], (r - n_x, t)
        )

    def across(src, a, zj, d):
        return remote(
            src,
            kv.at[a, zj * n_x + x],
            xs.at[d, a, zj],
            kvr.at[a, zj * n_x + x],
            (x_peers[d], t),
        )

    def kv_wait(a, j):
        remote(kv.at[a, j], kv.at[a, j], hs.at[0, 0], kvr.at[a, j], (r, sib)).wait_recv()

    for i in range(n_rc):
        h_other(i).start()
        h_sib(i).start()
    own = [pltpu.make_async_copy(hid.at[0], hbuf.at[t], loc_sem.at[0])]
    own.append(pltpu.make_async_copy(w_qkv, wq, loc_sem.at[1]))
    own.append(pltpu.make_async_copy(w_out, wo, loc_sem.at[2]))
    own.append(pltpu.make_async_copy(pk, kv.at[0, r], loc_sem.at[3]))
    own.append(pltpu.make_async_copy(pv, kv.at[1, r], loc_sem.at[4]))
    for a, src in ((0, pk), (1, pv)):

        @pl.when(z < n_z - 1)
        def _(a=a, src=src):
            up(src, a, z).start()

        @pl.when(z > 0)
        def _(a=a, src=src):
            down(src, a, z).start()

        for d in range(n_x - 1):
            across(src, a, z, d).start()
    for copy in own:
        copy.start()

    n_events = 2 * (n_z - 1)

    def handle(e):
        s, a = e // 2 + 1, e % 2

        @pl.when(z - s >= 0)
        def _():
            zj = z - s
            here = kv.at[a, zj * n_x + x]
            kv_wait(a, zj * n_x + x)

            @pl.when(z < n_z - 1)
            def _():
                up(here, a, zj).start()

            for d in range(n_x - 1):
                across(here, a, zj, d).start()

        @pl.when(z + s < n_z)
        def _():
            zj = z + s
            here = kv.at[a, zj * n_x + x]
            kv_wait(a, zj * n_x + x)

            @pl.when(z > 0)
            def _():
                down(here, a, zj).start()

            for d in range(n_x - 1):
                across(here, a, zj, d).start()

    length = length_ref[0]

    def live(i):
        ids = lax.broadcasted_iota(jnp.int32, (ROWS, width), 0) + i * ROWS
        return ids < length

    def cache_out(i, j):
        rows = rows_of(i)
        dst = (ck, cv)[j]
        return pltpu.make_async_copy(cst.at[j, rows], dst.at[0, rows], out_sem.at[j, i])

    own[0].wait()
    own[1].wait()

    def project(i, carry):
        rows = rows_of(i)
        h_other(i).wait_recv()
        h_fwd(i).start()
        h_sib(i).wait_recv()
        h_fwd(i).wait_recv()
        pieces = [hbuf[f, rows, :].astype(F32) for f in range(4)]
        mean = sum(jnp.sum(p, axis=1, keepdims=True) for p in pieces) * (1.0 / feats)
        pieces = [p - mean for p in pieces]
        var = sum(jnp.sum(p * p, axis=1, keepdims=True) for p in pieces) * (1.0 / feats)
        inv = 1.0 / jnp.sqrt(var + EPS)
        for f in range(4):
            cols = slice(f * width, (f + 1) * width)
            nrm[:, cols] = (pieces[f] * inv * gain[:, cols] + beta[:, cols]).astype(BF16)
        keep = live(i)
        for j in range(3):
            out = jnp.dot(nrm[...], wq[j], preferred_element_type=F32) + b_qkv[j : j + 1, :]
            out = out.astype(BF16)
            for h in range(heads):
                qkv[j, h, rows, :] = out[:, h * size : (h + 1) * size]
            if j > 0:
                cst[j - 1, rows, :] = jnp.where(keep, out, jnp.zeros_like(out))
                cache_out(i, j - 1).start()

        @pl.when(i < n_events)
        def _():
            handle(i)

        return carry

    lax.fori_loop(0, n_rc, project, 0)

    scale2 = LOG2E / math.sqrt(size)
    tri = lax.broadcasted_iota(jnp.int32, (ROWS, ROWS), 1) <= lax.broadcasted_iota(
        jnp.int32, (ROWS, ROWS), 0
    )

    def suffix(h, carry):
        slope2 = slope[h] * LOG2E
        ids = lax.broadcasted_iota(jnp.int32, (1, slots), 1)
        shift = jnp.where(ids < length, ids.astype(F32) * slope2, NEGATIVE)
        for i in range(n_rc):
            lo, hi = i * ROWS, (i + 1) * ROWS
            q = qkv[0, h, lo:hi, :]
            sd = dot_t(q, qkv[1, h, lo:hi, :]) * scale2 + shift[:, lo:hi]
            sd = jnp.where(tri, sd, NEGATIVE)
            m = jnp.max(sd, axis=1, keepdims=True)
            if i > 0:
                so = dot_t(q, qkv[1, h, 0:lo, :]) * scale2 + shift[:, 0:lo]
                m = jnp.maximum(m, jnp.max(so, axis=1, keepdims=True))
            wd = jnp.exp2(sd - m)
            total = jnp.sum(wd, axis=1, keepdims=True)
            out = jnp.dot(
                wd.astype(BF16), qkv[2, h, lo:hi, :], preferred_element_type=F32
            )
            if i > 0:
                wo_ = jnp.exp2(so - m)
                total = total + jnp.sum(wo_, axis=1, keepdims=True)
                out = out + jnp.dot(
                    wo_.astype(BF16), qkv[2, h, 0:lo, :], preferred_element_type=F32
                )
            acc[h, lo:hi, :] = out
            mst[h, lo:hi, :] = jnp.broadcast_to(m, (ROWS, size))
            lst[h, lo:hi, :] = jnp.broadcast_to(total, (ROWS, size))

        @pl.when(n_rc + h < n_events)
        def _():
            handle(n_rc + h)

        return carry

    lax.fori_loop(0, heads, suffix, 0)

    def late(e, carry):
        handle(e)
        return carry

    if n_events > n_rc + heads:
        lax.fori_loop(n_rc + heads, n_events, late, 0)

    for copy in own[2:]:
        copy.wait()

    def wait_across(zj, carry):
        for a in range(2):
            for d in range(1, n_x):
                kv_wait(a, zj * n_x + (x + d) % n_x)
        return carry

    lax.fori_loop(0, n_z, wait_across, 0)

    def wait_number(d, carry):
        j = (r + d) % n_req
        remote(ids.at[j], ids.at[j], hs.at[0, 0], ids_recv.at[j], (r, sib)).wait_recv()
        number(d).wait_send()
        return carry

    lax.fori_loop(1, n_req, wait_number, 0)
    first = group_ref[0] * nb

    def to_sib(i):
        return remote(pbuf.at[i, 1 - c], sibr.at[i], ss.at[i], sr.at[i], (r, sib))

    def to_oth(i):
        return remote(ys.at[i], yr.at[i], yss.at[i], yrs.at[i], (r, oth))

    step = 4
    inner = lax.broadcasted_iota(jnp.int32, (1, block), 1) - prefix

    def local_number(j):
        row = ids[j, 0:1, :] - first
        return jnp.concatenate([row] * (block // row.shape[1]), axis=1)

    def shift_of(j):
        return (local_number(j) * block + inner).astype(F32)

    def veil_of(j):
        number = local_number(j)
        return jnp.where((number >= 0) & (number < nb), 0.0, NEGATIVE)

    def finish(i, carry):
        rows = rows_of(i)
        for h in range(heads):
            slope2 = slope[h] * LOG2E
            cols = slice(h * size, (h + 1) * size)
            q = qkv[0, h, rows, :]
            m = mst[h, rows, :][:, :1]
            total = lst[h, rows, :][:, :1]
            out = acc[h, rows, :]

            def fold(g, state):
                m, total, out = state
                holders = [g * step + k for k in range(step)]
                keys = jnp.concatenate([kv[0, j, :, cols] for j in holders], axis=0)
                vals = jnp.concatenate([kv[1, j, :, cols] for j in holders], axis=0)
                shift = [shift_of(j) * slope2 + veil_of(j) for j in holders]
                sc = dot_t(q, keys) * scale2 + jnp.concatenate(shift, axis=1)
                new = jnp.maximum(m, jnp.max(sc, axis=1, keepdims=True))
                fac = jnp.exp2(m - new)
                w = jnp.exp2(sc - new)
                total = total * fac + jnp.sum(w, axis=1, keepdims=True)
                out = out * fac + jnp.dot(w.astype(BF16), vals, preferred_element_type=F32)
                return new, total, out

            state = (m, total, out)
            if n_req <= 2 * step:
                for g in range(n_req // step):
                    state = fold(g, state)
            else:
                state = lax.fori_loop(0, n_req // step, fold, state)
            m, total, out = state
            att[:, cols] = (out / total).astype(BF16)
        for f in range(4):
            part = jnp.dot(
                att[...], wo[:, f * width : (f + 1) * width], preferred_element_type=F32
            )
            pbuf[i, f % 2, f // 2] = part.astype(BF16)
        to_sib(i).start()
        to_sib(i).wait_recv()
        ys[i] = (pbuf[i, c, 1 - y].astype(F32) + sibr[i, 1 - y].astype(F32)).astype(BF16)
        to_oth(i).start()
        return carry

    lax.fori_loop(0, n_rc, finish, 0)

    def mixed_out(i):
        rows = rows_of(i)
        return pltpu.make_async_copy(ost.at[rows], mixed.at[0, rows], out_sem.at[2, i])

    def final(i, carry):
        rows = rows_of(i)
        to_oth(i).wait_recv()
        out = pbuf[i, c, y].astype(F32) + sibr[i, y].astype(F32) + yr[i].astype(F32)
        out = out + b_out[t] + hbuf[t, rows, :].astype(F32)
        ost[rows, :] = jnp.where(live(i), out, 0.0).astype(BF16)
        mixed_out(i).start()
        return carry

    lax.fori_loop(0, n_rc, final, 0)

    def drain(i, carry):
        h_other(i).wait_send()
        h_sib(i).wait_send()
        h_fwd(i).wait_send()
        to_sib(i).wait_send()
        to_oth(i).wait_send()
        cache_out(i, 0).wait()
        cache_out(i, 1).wait()
        mixed_out(i).wait()
        return carry

    lax.fori_loop(0, n_rc, drain, 0)

    def drain_prefix(zj, carry):
        for a in range(2):
            here = kv.at[a, zj * n_x + x]

            @pl.when(jnp.logical_and(zj <= z, z < n_z - 1))
            def _():
                up(here, a, zj).wait_send()

            @pl.when(jnp.logical_and(zj >= z, z > 0))
            def _():
                down(here, a, zj).wait_send()

            for d in range(n_x - 1):
                across(here, a, zj, d).wait_send()
        return carry

    lax.fori_loop(0, n_z, drain_prefix, 0)


def on_device(
    n_req,
    n_x,
    hidden_in,
    ln_gain,
    ln_bias,
    w_qkv,
    b_qkv,
    w_out,
    b_out,
    alibi_slope,
    prefix_k,
    prefix_v,
    suffix_len,
    group_of,
    block_of_device,
):
    _, slots, width = hidden_in.shape
    heads = alibi_slope.shape[0]
    size = w_qkv.shape[2] // heads
    block = prefix_k.shape[0]
    n_rc = slots // ROWS
    n_z = n_req // n_x
    smem = pl.BlockSpec(memory_space=pltpu.SMEM)
    vmem = pl.BlockSpec(memory_space=pltpu.VMEM)
    hbm = pl.BlockSpec(memory_space=pltpu.HBM)
    anywhere = pl.BlockSpec(memory_space=pl.ANY)
    dma = pltpu.SemaphoreType.DMA
    cache = jax.ShapeDtypeStruct((1, slots, width), BF16)
    return pl.pallas_call(
        functools.partial(kernel, n_req, n_x),
        out_shape=(cache, cache, cache),
        in_specs=[smem, smem, smem, smem, hbm, vmem, vmem, hbm, vmem, hbm, vmem, hbm, hbm],
        out_specs=(anywhere, anywhere, anywhere),
        scratch_shapes=[
            pltpu.VMEM((4, slots, width), BF16),
            pltpu.VMEM(w_qkv.shape, BF16),
            pltpu.VMEM(w_out.shape, BF16),
            pltpu.VMEM((ROWS, 4 * width), BF16),
            pltpu.VMEM((3, heads, slots, size), BF16),
            pltpu.VMEM((2, slots, width), BF16),
            pltpu.VMEM((2, n_req, block, heads * size), BF16),
            pltpu.VMEM((heads, slots, size), F32),
            pltpu.VMEM((heads, slots, size), F32),
            pltpu.VMEM((heads, slots, size), F32),
            pltpu.VMEM((ROWS, heads * size), BF16),
            pltpu.VMEM((n_rc, 2, 2, ROWS, width), BF16),
            pltpu.VMEM((n_rc, 2, ROWS, width), BF16),
            pltpu.VMEM((n_rc, ROWS, width), BF16),
            pltpu.VMEM((n_rc, ROWS, width), BF16),
            pltpu.VMEM((slots, width), BF16),
            pltpu.VMEM((n_req, 8, 128), jnp.int32),
            pltpu.VMEM((8, 128), jnp.int32),
            dma((5,)),
            dma((3, n_rc)),
            dma((3, n_rc)),
            dma((3, n_rc)),
            dma((2, 2, n_z)),
            dma((n_x - 1, 2, n_z)),
            dma((2, n_req)),
            dma((n_rc,)),
            dma((n_rc,)),
            dma((n_rc,)),
            dma((n_rc,)),
            dma((n_req,)),
            dma((n_req,)),
        ],
        compiler_params=pltpu.CompilerParams(
            collective_id=0, has_side_effects=True, vmem_limit_bytes=(42 << 20) + 4 * n_req * block * width
        ),
        name="sublayer",
    )(
        block_of_device,
        group_of,
        suffix_len,
        alibi_slope,
        hidden_in,
        ln_gain[None],
        ln_bias[None],
        w_qkv,
        b_qkv,
        w_out,
        b_out.reshape(4, 1, width),
        prefix_k,
        prefix_v,
    )


def solution(mesh):
    n_req = mesh.shape["req"]
    n_x = 2 if n_req <= 8 else 4
    return jax.shard_map(
        functools.partial(on_device, n_req, n_x),
        mesh=mesh,
        in_specs=(
            P("req", None, "tp"),
            P(),
            P(),
            P(None, None, "tp"),
            P(None, "tp"),
            P("tp", None),
            P(),
            P("tp"),
            P("req", "tp"),
            P("req", "tp"),
            P("req"),
            P("req"),
            P("req"),
        ),
        out_specs=(P("req", None, "tp"), P("req", None, "tp"), P("req", None, "tp")),
        check_vma=False,
    )
```
